1024 devices in a mesh: vir: 128 (over z_hi, x, y, core), out: 8 (over z_lo).
Axes of the slice: x: 4, y: 8, z: 16 (z_hi: 2, z_lo: 8; z = z_hi * 8 + z_lo), core: 2. Of those that a mesh axis runs over, the one named last changes fastest.
Arguments:
- factors: bfloat16 [512, 512, 1536], P('out', 'vir'), may hold values from -2.5 to 2.5
- amplitudes: bfloat16 [128, 512, 512], P('out', 'vir'), may hold values from -0.046875 to 0.046875
Outputs:
- ladder: float32 [2, 128, 512], P(None, 'vir', 'out')
The draws below stay inside these ranges and needn't reach their ends.
All inputs are finite; a program needn't handle non-finite values.
Results may differ from the reference program's by a relative error of at most 0.0029.
Values may be sent and summed in bfloat16 or wider, within the bound.
A program may use at most 32 MiB of HBM per device.

```python
import jax
import jax.numpy as jnp
from jax import lax

V = 512
NAUX = 1536
PAIRS = 128
BB = 2


def raised(drawn, key, source, target, blocks, factor):
    def block_of(axis_at):
        return (jnp.arange(drawn.shape[axis_at]) // (drawn.shape[axis_at] // blocks)).reshape((-1,) + (1,) * (drawn.ndim - 1 - axis_at))

    one_side = jax.random.permutation(key, blocks)[block_of(target)]
    second = (block_of(target) + blocks // 2) % blocks
    return jnp.where((block_of(source) == one_side) | (block_of(source) == second), factor * drawn, drawn)


def shard_levels(rng, extent, pieces, smallest, largest):
    factor_of = 1.0
    for dim, parts in pieces:
        steps = jax.random.uniform(jax.random.fold_in(jax.random.fold_in(rng, 6), dim), (parts,), jnp.float32, smallest / len(pieces), largest / len(pieces))
        factor_of = factor_of * jnp.repeat(jnp.exp(steps), extent[dim] // parts).reshape((-1,) + (1,) * (len(extent) - 1 - dim))
    return factor_of


def bell_draw(own_key, dims, scale, limit, split=(), held_as=jnp.bfloat16):
    values = jax.random.normal(own_key, dims, jnp.float32) * scale
    if len(split) > 0:
        values = shard_levels(own_key, dims, split, -0.22, 0.18) * values
    return jnp.clip(values, min=-limit, max=limit).astype(held_as)


def noise_with(key, extent, spread, bound, pieces, heavy, kind=jnp.bfloat16):
    drawn = spread * jax.random.normal(key, extent, jnp.float32)
    if pieces:
        drawn = drawn * shard_levels(key, extent, pieces, -0.22, 0.18)
    return jnp.clip(raised(drawn, jax.random.fold_in(key, 3), *heavy), -bound, bound).astype(kind)


def setup_inputs(seed: int = 0) -> dict:
    streams_of = jax.random.split(jax.random.key(seed), 3)
    return {
        "factors": bell_draw(streams_of[0], (V, V, NAUX), 0.16, 2.5, ((0, 8), (1, 128))),
        "amplitudes": noise_with(streams_of[1], (PAIRS, V, V), 0.002, 0.046875, ((0, 8), (1, 128)), (1, 0, 128, 5.5)),
    }


def reference(factors, amplitudes):
    slab_rows = factors[:BB].astype(jnp.float32).reshape(BB * V, NAUX)
    amplitude_rows = amplitudes.astype(jnp.float32).reshape(PAIRS, V * V)
    block_len = min(64, V)

    def per_block(factor_block):
        tiles = jnp.dot(factor_block.astype(jnp.float32).reshape(block_len * V, NAUX), slab_rows.T)
        tiles = lax.optimization_barrier(tiles.astype(jnp.bfloat16)).astype(jnp.float32)
        tiles = tiles.reshape(block_len, V, BB, V).transpose(0, 2, 1, 3).reshape(block_len * BB, V * V)
        result = jnp.dot(tiles, amplitude_rows.T)
        return result.reshape(block_len, BB, PAIRS)

    blocks = lax.map(per_block, factors.reshape(V // block_len, block_len, V, NAUX))
    return blocks.reshape(V, BB, PAIRS).transpose(1, 2, 0)
```

```python
import jax
import jax.numpy as jnp
from jax import lax
from jax.experimental import pallas as pl
from jax.experimental.pallas import tpu as pltpu
from jax.sharding import Mesh
from jax.sharding import PartitionSpec as P

ZH, X, Y, CORE, ZL = "vir_0", "vir_1", "vir_2", "vir_3", "out"
VIR = (ZH, X, Y, CORE)
NZH, NX, NY, NC, NZL = 2, 4, 8, 2, 8
BB, NCV, NA, AUX, V, PAIRS = 2, 4, 64, 1536, 512, 128
MESH = pl.DeviceIdType.MESH
BF, F32 = jnp.bfloat16, jnp.float32


def kernel(
    f_ref, t_ref, o_ref,
    piece, slab, traw, fm, tm, te, integ, r0, ra, rbs, rb,
    local_sem, z_send, z_recv, t_send, t_recv, xn_send, xn_recv, yr_send, yr_recv,
    yf_send, yf_recv, xf_send, xf_recv, pn_send, pn_recv, pf_send, pf_recv,
    ra_send, ra_recv, rb_send, rb_recv,
):
    zh, x, y, h, zl = (lax.axis_index(n) for n in (ZH, X, Y, CORE, ZL))
    near = jnp.where(zl <= NZL // 2, zh, 1 - zh)
    sends = []

    def put(src, dst, ssem, rsem, **where):
        copy = pltpu.make_async_remote_copy(
            src_ref=src, dst_ref=dst, send_sem=ssem, recv_sem=rsem,
            device_id={names[k]: v for k, v in where.items()}, device_id_type=MESH,
        )
        copy.start()
        return copy

    names = {"zh": ZH, "x": X, "y": Y, "h": CORE, "zl": ZL}

    def arrived(dst, rsem):
        pltpu.make_async_copy(dst, dst, rsem).wait()

    def left(src, ssem):
        pltpu.make_async_copy(src, src, ssem).wait()

    barrier = pltpu.get_barrier_semaphore()

    def greet(**where):
        pl.semaphore_signal(
            barrier, inc=1, device_id={names[k]: v for k, v in where.items()}, device_id_type=MESH
        )

    idx_z = zh * NZL + zl
    for o in range(1, 16):
        other = lax.rem(idx_z + o, 16)
        greet(zh=other // NZL, zl=lax.rem(other, NZL))
    idx_a = h * NX + x
    for o in range(1, 8):
        other = lax.rem(idx_a + o, 8)
        greet(h=other // NX, x=lax.rem(other, NX))
    for o in range(1, NY):
        greet(y=lax.rem(y + o, NY))

    piece[0:4, :] = f_ref[0]
    piece[4:8, :] = f_ref[1]
    for c in range(NCV):
        fm[c * NA : (c + 1) * NA, :] = f_ref[:, c, :]

    pl.semaphore_wait(barrier, 15 + 7 + 7)

    def z_place(n):
        group = jnp.where(n == 0, 7, NZL + y // 4)
        inner = jnp.where(n == 0, x, lax.rem(y, 4))
        return slab.at[group, inner, h]

    @pl.when(zl == 0)
    def _():
        pltpu.make_async_copy(piece, z_place(0), local_sem.at[0]).start()
        for o in (8, 7, 9, 6, 10, 5, 11, 4, 12, 3, 13, 2, 14, 1, 15):
            other = lax.rem(idx_z + o, 16)
            ozh, ozl = other // NZL, lax.rem(other, NZL)
            onear = jnp.where(ozl <= NZL // 2, ozh, 1 - ozh)
            n = jnp.where(onear == zh, 0, 1)
            put(piece, z_place(n), z_send.at[o - 1], z_recv.at[n], zh=ozh, zl=ozl)
        pltpu.make_async_copy(piece, z_place(0), local_sem.at[0]).wait()

    @pl.when(zl != 0)
    def _():
        arrived(piece, z_recv.at[0])

    for o in range(1, NX):
        put(slab.at[7, x, h], slab.at[7, x, h], xn_send.at[o - 1], xn_recv.at[o - 1], x=lax.rem(x + o, NX))
    for o in range(1, NX):
        arrived(slab.at[7, x, h], xn_recv.at[o - 1])

    up, down = lax.rem(y + 1, NY), lax.rem(y + NY - 1, NY)

    def near_part(pos):
        return slab.at[pos, :, h]

    def ring(k, src, up_pos, down_pos):
        put(near_part(src[0]), near_part(up_pos), yr_send.at[2 * k], yr_recv.at[up_pos], y=up)
        put(near_part(src[1]), near_part(down_pos), yr_send.at[2 * k + 1], yr_recv.at[down_pos], y=down)

    def share_near(pos):
        put(near_part(pos), near_part(pos), pn_send.at[pos], pn_recv.at[pos], h=1 - h)

    ring(0, (7, 7), 0, 1)
    share_near(7)

    arrived(piece, z_recv.at[1])
    far = slab.at[NZL + y // 4, lax.rem(y, 4), h]
    for o in (4, 3, 5, 2, 6, 1, 7):
        put(far, far, yf_send.at[o - 1], yf_recv.at[o - 1], y=lax.rem(y + o, NY))

    pltpu.make_async_copy(t_ref, traw.at[zl], local_sem.at[0]).start()
    for o in range(1, NZL):
        put(t_ref, traw.at[zl], t_send.at[o - 1], t_recv.at[o - 1], zl=lax.rem(zl + o, NZL))
    pltpu.make_async_copy(t_ref, traw.at[zl], local_sem.at[0]).wait()

    def multiply(g):
        rows = slab[2 * g : 2 * g + 2].reshape(128, AUX)
        tile = lax.dot_general(fm[...], rows, (((1,), (1,)), ((), ())), preferred_element_type=F32)
        integ[:, g * 128 : (g + 1) * 128] = tile.astype(BF)

    for pos in (0, 1):
        arrived(near_part(pos), yr_recv.at[pos])
    ring(1, (0, 1), 2, 3)
    share_near(0)
    share_near(1)

    def far_part(k):
        return slab.at[NZL + 2 * k : NZL + 2 * k + 2, :, h]

    for o in range(1, NY):
        arrived(far, yf_recv.at[o - 1])
    for o in (2, 1, 3):
        k = NX - o
        put(far_part(0), far_part(k), xf_send.at[o - 1], xf_recv.at[k - 1], x=lax.rem(x + o, NX))
    put(far_part(0), far_part(0), pf_send.at[0], pf_recv.at[0], h=1 - h)

    for pos in (2, 3):
        arrived(near_part(pos), yr_recv.at[pos])
    ring(2, (2, 3), 4, 5)
    share_near(2)
    share_near(3)

    for pos in (4, 5):
        arrived(near_part(pos), yr_recv.at[pos])
    put(slab.at[4, 0:2, h], slab.at[6, 0:2, h], yr_send.at[6], yr_recv.at[6], y=up)
    put(slab.at[5, 2:4, h], slab.at[6, 2:4, h], yr_send.at[7], yr_recv.at[7], y=down)
    share_near(4)
    share_near(5)

    for pos in (0, 1):
        arrived(near_part(pos), pn_recv.at[pos])
    multiply(0)
    for pos in (2, 3):
        arrived(near_part(pos), pn_recv.at[pos])
    multiply(1)
    arrived(slab.at[6, 0:2, h], yr_recv.at[6])
    arrived(slab.at[6, 2:4, h], yr_recv.at[7])
    share_near(6)
    for pos in (4, 5):
        arrived(near_part(pos), pn_recv.at[pos])
    multiply(2)
    arrived(far_part(0), pf_recv.at[0])
    multiply(4)
    for k in (1, 3, 2):
        arrived(far_part(k), xf_recv.at[k - 1])
        put(far_part(k), far_part(k), pf_send.at[k], pf_recv.at[k], h=1 - h)
    for pos in (6, 7):
        arrived(near_part(pos), pn_recv.at[pos])
    multiply(3)

    for o in range(1, NZL):
        arrived(t_ref, t_recv.at[o - 1])
    for s in range(NZL):
        szh, sx = s // NX, s % NX
        for core in range(NC):
            for c in range(NCV):
                row = c * 128 + core * 64 + sx * 16 + szh * 8
                tm[row : row + 8, :] = traw[s, :, core, c, :]
    for g in range(8):
        j = lax.broadcasted_iota(jnp.int32, (V, 128), 1) + g * 128
        d = lax.broadcasted_iota(jnp.int32, (V, 128), 0)
        pos, xx, core, b, i = j // 64, (j // 16) % 4, (j // 8) % 2, (j // 4) % 2, j % 4
        if g < 4:
            step = jnp.where(pos % 2 == 0, NY - 1 - pos // 2, pos // 2 + 1)
            yy = lax.rem(jnp.where(pos == 7, 0, step) + y, NY)
            src = ((near * NX + xx) * NY + yy) * NC + core
        else:
            yy = (pos % 2) * 4 + xx
            src = (((1 - near) * NX + lax.rem(x + g - 4, NX)) * NY + yy) * NC + core
        hit = src * NCV + i == d
        both = jnp.concatenate([jnp.where(hit & (b == n), 1.0, 0.0).astype(BF) for n in range(BB)], axis=1)
        spread = jnp.dot(tm[...], both, preferred_element_type=F32).astype(BF)
        for n in range(BB):
            te[n, :, g * 128 : (g + 1) * 128] = spread[:, n * 128 : (n + 1) * 128]

    for k in (1, 3, 2):
        arrived(far_part(k), pf_recv.at[k])
        multiply(4 + k)

    terms = []
    for n in range(BB):
        acc = jnp.zeros((PAIRS, NA), F32)
        for c in range(NCV):
            acc += lax.dot_general(
                te[n, c * 128 : (c + 1) * 128, :], integ[c * NA : (c + 1) * NA, :],
                (((1,), (1,)), ((), ())), preferred_element_type=F32,
            )
        terms.append(acc)
    r0[...] = jnp.concatenate(terms, axis=1).reshape(8, NZH, NY, 128)

    for o in range(1, 8):
        other = lax.rem(idx_a + o, 8)
        put(r0.at[other], ra.at[o - 1], ra_send.at[o - 1], ra_recv.at[o - 1], h=other // NX, x=lax.rem(other, NX))
    part = r0[idx_a]
    for o in range(1, 8):
        arrived(ra.at[o - 1], ra_recv.at[o - 1])
    for o in range(1, 8):
        part += ra[o - 1]
    for q in range(16):
        rbs[q] = part[q // NY, q % NY : q % NY + 1, :]
    idx_b = zh * NY + y
    for o in (8, 12, 4, 7, 9, 11, 13, 5, 3, 6, 10, 14, 2, 15, 1):
        other = lax.rem(idx_b + o, 16)
        put(rbs.at[other], rb.at[o - 1], rb_send.at[o - 1], rb_recv.at[o - 1], zh=other // NY, y=lax.rem(other, NY))
    total = rbs[idx_b]
    for o in range(1, 16):
        arrived(rb.at[o - 1], rb_recv.at[o - 1])
    for o in range(1, 16):
        total += rb[o - 1]
    o_ref[...] = total

    @pl.when(zl == 0)
    def _():
        for o in range(15):
            left(piece, z_send.at[o])
    for o in range(NZL - 1):
        left(t_ref, t_send.at[o])
    for o in range(NX - 1):
        left(slab.at[7, x, h], xn_send.at[o])
        left(far_part(0), xf_send.at[o])
    for k in range(6):
        left(near_part(0), yr_send.at[k])
    for k in (6, 7):
        left(slab.at[4, 0:2, h], yr_send.at[k])
    for o in range(NY - 1):
        left(far, yf_send.at[o])
    for pos in range(8):
        left(near_part(pos), pn_send.at[pos])
    for k in range(4):
        left(far_part(k), pf_send.at[k])
    for o in range(7):
        left(r0.at[0], ra_send.at[o])
    for o in range(15):
        left(rbs.at[0], rb_send.at[o])


def body(factors, amplitudes):
    dma = pltpu.SemaphoreType.DMA
    row = pl.pallas_call(
        kernel,
        out_shape=jax.ShapeDtypeStruct((1, BB * NA), F32),
        in_specs=[pl.BlockSpec(memory_space=pltpu.VMEM)] * 2,
        out_specs=pl.BlockSpec(memory_space=pltpu.VMEM),
        scratch_shapes=[
            pltpu.VMEM((8, AUX), BF),
            pltpu.VMEM((16, 4, NC, 8, AUX), BF),
            pltpu.VMEM((NZL, NY, NC, NCV, V), BF),
            pltpu.VMEM((NCV * NA, AUX), BF),
            pltpu.VMEM((NCV * PAIRS, V), BF),
            pltpu.VMEM((BB, NCV * PAIRS, 1024), BF),
            pltpu.VMEM((NCV * NA, 1024), BF),
            pltpu.VMEM((8, NZH, NY, 128), F32),
            pltpu.VMEM((7, NZH, NY, 128), F32),
            pltpu.VMEM((16, 1, 128), F32),
            pltpu.VMEM((15, 1, 128), F32),
            dma((1,)), dma((15,)), dma((2,)), dma((7,)), dma((7,)), dma((3,)), dma((3,)), dma((8,)), dma((8,)),
            dma((7,)), dma((7,)), dma((3,)), dma((3,)), dma((8,)), dma((8,)), dma((4,)), dma((4,)),
            dma((7,)), dma((7,)), dma((15,)), dma((15,)),
        ],
        compiler_params=pltpu.CompilerParams(collective_id=0, has_side_effects=True),
    )(factors, amplitudes.reshape(NY, NC, NCV, V))
    return row.reshape(BB, 1, NA)


def solution(mesh):
    torus = Mesh(mesh.devices.reshape(NZH, NX, NY, NC, NZL), (ZH, X, Y, CORE, ZL))
    in_specs = (P(ZL, VIR, None), P(ZL, VIR, None))
    return jax.shard_map(body, mesh=torus, in_specs=in_specs, out_specs=P(None, VIR, ZL), check_vma=False)
```

```python
import jax
import jax.numpy as jnp
from jax import lax
from jax.experimental import pallas as pl
from jax.experimental.pallas import tpu as pltpu
from jax.sharding import Mesh
from jax.sharding import PartitionSpec as P

ZH, X, Y, CORE, ZL = "vir_0", "vir_1", "vir_2", "vir_3", "out"
VIR = (ZH, X, Y, CORE)
NZH, NX, NY, NC, NZL = 2, 4, 8, 2, 8
BB, NCV, NA, AUX, V, PAIRS = 2, 4, 64, 1536, 512, 128
MESH = pl.DeviceIdType.MESH
BF, F32 = jnp.bfloat16, jnp.float32


def kernel(
    f_ref, t_ref, o_ref,
    piece, slab, traw, fm, tm, pick, te, integ, r0, ra, rbs, rb,
    local_sem, mid_sem, z_send, z_recv, t_send, t_recv, xn_send, xn_recv, yr_send, yr_recv,
    yf_send, yf_recv, xf_send, xf_recv, pn_send, pn_recv, pf_send, pf_recv,
    ra_send, ra_recv, rb_send, rb_recv,
):
    zh, x, y, h, zl = (lax.axis_index(n) for n in (ZH, X, Y, CORE, ZL))
    near = jnp.where(zl <= NZL // 2, zh, 1 - zh)
    names = {"zh": ZH, "x": X, "y": Y, "h": CORE, "zl": ZL}

    def to(where):
        return dict(device_id={names[k]: v for k, v in where.items()}, device_id_type=MESH)

    def put(src, dst, ssem, rsem, **where):
        pltpu.make_async_remote_copy(src_ref=src, dst_ref=dst, send_sem=ssem, recv_sem=rsem, **to(where)).start()

    def arrived(dst, rsem):
        pltpu.make_async_copy(dst, dst, rsem).wait()

    left = arrived

    barrier = pltpu.get_barrier_semaphore()
    idx_z = zh * NZL + zl
    idx_a = h * NX + x
    idx_b = zh * NY + y

    def at_z(o):
        other = lax.rem(idx_z + o + 16, 16)
        return dict(zh=other // NZL, zl=lax.rem(other, NZL))

    def at_a(o):
        other = lax.rem(idx_a + o, 8)
        return other, dict(h=other // NX, x=lax.rem(other, NX))

    for o in (-4, 4, -3, 3, -2, 2, -1, 1):
        pl.semaphore_signal(barrier, inc=1, **to(at_z(o)))
    for o in range(1, 8):
        pl.semaphore_signal(barrier, inc=1, **to(at_a(o)[1]))
    for o in range(1, NY):
        pl.semaphore_signal(barrier, inc=1, **to(dict(y=lax.rem(y + o, NY))))

    piece[0:4, :] = f_ref[0]
    piece[4:8, :] = f_ref[1]
    own_t = pltpu.make_async_copy(t_ref, traw.at[zl], local_sem.at[0])
    own_t.start()
    for c in range(NCV):
        fm[c * NA : (c + 1) * NA, :] = f_ref[:, c, :]

    pl.semaphore_wait(barrier, 8 + 7 + 7)
    pl.semaphore_signal(mid_sem, inc=1, **to(at_z(-4)))

    near_own, far_own = slab.at[7, x, h], slab.at[8, 2, h]

    @pl.when(zl == 0)
    def _():
        own = pltpu.make_async_copy(piece, near_own, local_sem.at[1])
        own.start()
        put(piece, near_own, z_send.at[0], z_recv.at[0], **at_z(4))
        put(piece, far_own, z_send.at[1], z_recv.at[1], **at_z(-4))
        for s, o in enumerate((3, -3, 2, -2, 1, -1)):
            put(piece, near_own, z_send.at[2 + s], z_recv.at[0], **at_z(o))
        own.wait()

    @pl.when(zl != 0)
    def _():
        arrived(near_own, z_recv.at[0])

    @pl.when(zl == 4)
    def _():
        for s, o in enumerate((4, 3, 2, 1)):
            put(near_own, far_own, z_send.at[s], z_recv.at[1], **at_z(o))

    for o in range(1, NX):
        put(near_own, near_own, xn_send.at[o - 1], xn_recv.at[o - 1], x=lax.rem(x + o, NX))

    mate = lax.rem(zl + 4, NZL)
    quad = [(zl // 4) * 4 + lax.rem(zl + o, 4) for o in range(1, 4)]

    def amplitudes_out():
        put(t_ref, traw.at[zl], t_send.at[0], t_recv.at[0], zl=mate)
        for o in range(3):
            put(t_ref, traw.at[zl], t_send.at[1 + o], t_recv.at[1 + o], zl=quad[o])

    def amplitudes_on():
        arrived(t_ref, t_recv.at[0])
        for o in range(3):
            put(traw.at[mate], traw.at[mate], t_send.at[4 + o], t_recv.at[4 + o], zl=quad[o])

    up, down = lax.rem(y + 1, NY), lax.rem(y + NY - 1, NY)
    xup, xdown = lax.rem(x + 1, NX), lax.rem(x + NX - 1, NX)

    def near_part(pos):
        return slab.at[pos, :, h]

    def near_half(pos, f):
        return slab.at[pos, 2 * f : 2 * f + 2, h]

    def ring(src, dst, f, y_to):
        s = 2 * dst + f
        put(near_half(src, f), near_half(dst, f), yr_send.at[s], yr_recv.at[s], y=y_to)

    def ring_arrived(pos, f):
        arrived(near_half(pos, f), yr_recv.at[2 * pos + f])

    def share_near(pos):
        put(near_part(pos), near_part(pos), pn_send.at[pos], pn_recv.at[pos], h=1 - h)

    def near_shared(pos):
        arrived(near_part(pos), pn_recv.at[pos])

    def far_half(k, c):
        return slab.at[8 + 2 * k + c, :, h]

    def far_on(src, dst, c, x_to):
        s = 2 * dst + c - 2
        put(far_half(src, c), far_half(dst, c), xf_send.at[s], xf_recv.at[s], x=x_to)

    def far_arrived(k, c):
        arrived(far_half(k, c), xf_recv.at[2 * k + c - 2])

    def share_far(k, c):
        s = 2 * k + c
        put(far_half(k, c), far_half(k, c), pf_send.at[s], pf_recv.at[s], h=1 - h)

    def far_shared(k):
        for c in range(2):
            arrived(far_half(k, c), pf_recv.at[2 * k + c])

    def multiply(g):
        rows = slab[2 * g : 2 * g + 2].reshape(128, AUX)
        tile = lax.dot_general(fm[...], rows, (((1,), (1,)), ((), ())), preferred_element_type=F32)
        integ[:, g * 128 : (g + 1) * 128] = tile.astype(BF)

    amplitudes_out()
    for o in range(1, NX):
        arrived(near_own, xn_recv.at[o - 1])
    for f in range(2):
        ring(7, 0, f, up)
        ring(7, 1, f, down)
    share_near(7)

    arrived(far_own, z_recv.at[1])

    @pl.when(zl == 4)
    def _():
        for s, o in enumerate((-3, -2, -1)):
            put(far_own, far_own, z_send.at[4 + s], z_recv.at[1], **at_z(o))

    pl.semaphore_wait(mid_sem, 1)
    for o in (7, 1, 2, 6, 3, 5, 4):
        q = (2 - o) % NY
        put(far_own, slab.at[8 + q // 4, q % 4, h], yf_send.at[o - 1], yf_recv.at[o - 1], y=lax.rem(y + o, NY))

    for step in range(2):
        for f in range(2):
            ring_arrived(2 * step, f)
            ring(2 * step, 2 * step + 2, f, up)
            ring_arrived(2 * step + 1, f)
            ring(2 * step + 1, 2 * step + 3, f, down)
        share_near(2 * step)
        share_near(2 * step + 1)
        for o in ((1, 2, 7), (3, 4, 5, 6))[step]:
            arrived(far_own, yf_recv.at[o - 1])
        far_on(0, 3, step, xup)
        far_on(0, 1, step, xdown)
        share_far(0, step)

    d = lax.broadcasted_iota(jnp.int32, (V, 128), 0)
    for g in range(8):
        j = lax.broadcasted_iota(jnp.int32, (1, 128), 1) + g * 128
        pos, xx, core, b, i = j // 64, (j // 16) % 4, (j // 8) % 2, (j // 4) % 2, j % 4
        if g < 4:
            step = jnp.where(pos % 2 == 0, NY - 1 - pos // 2, pos // 2 + 1)
            yy = lax.rem(jnp.where(pos == 7, 0, step) + y, NY)
            src = ((near * NX + xx) * NY + yy) * NC + core
        else:
            yy = lax.rem((pos % 2) * 4 + xx + y + NY - 2, NY)
            src = (((1 - near) * NX + lax.rem(x + g - 4, NX)) * NY + yy) * NC + core
        for n in range(BB):
            want = jnp.where(b == n, src * NCV + i, -1)
            pick[g, :, n * 128 : (n + 1) * 128] = jnp.where(d == want, 1.0, 0.0).astype(BF)

    amplitudes_on()
    near_shared(0)
    near_shared(1)
    multiply(0)

    ring_arrived(4, 0)
    ring(4, 6, 0, up)
    ring_arrived(5, 1)
    ring(5, 6, 1, down)
    ring_arrived(4, 1)
    ring_arrived(5, 0)
    share_near(4)
    share_near(5)
    far_arrived(3, 0)
    far_on(3, 2, 0, xup)
    share_far(3, 0)
    far_arrived(1, 0)
    share_far(1, 0)
    near_shared(2)
    near_shared(3)
    multiply(1)
    far_arrived(1, 1)
    far_on(1, 2, 1, xdown)
    share_far(1, 1)
    far_arrived(3, 1)
    share_far(3, 1)
    near_shared(4)
    near_shared(5)
    multiply(2)
    ring_arrived(6, 0)
    ring_arrived(6, 1)
    share_near(6)
    far_shared(0)
    multiply(4)
    for c in range(2):
        far_arrived(2, c)
        share_far(2, c)

    own_t.wait()
    for o in range(1, NZL - 1):
        arrived(t_ref, t_recv.at[o])
    for s in range(NZL):
        szh, sx = s // NX, s % NX
        for core in range(NC):
            for c in range(NCV):
                row = c * 128 + core * 64 + sx * 16 + szh * 8
                tm[row : row + 8, :] = traw[s, :, core, c, :]
    for g in range(8):
        spread = jnp.dot(tm[...], pick[g], preferred_element_type=F32).astype(BF)
        for n in range(BB):
            te[n, :, g * 128 : (g + 1) * 128] = spread[:, n * 128 : (n + 1) * 128]

    near_shared(6)
    near_shared(7)
    multiply(3)
    for k in (1, 3, 2):
        far_shared(k)
        multiply(4 + k)

    terms = []
    for n in range(BB):
        acc = jnp.zeros((PAIRS, NA), F32)
        for c in range(NCV):
            acc += lax.dot_general(
                te[n, c * 128 : (c + 1) * 128, :], integ[c * NA : (c + 1) * NA, :],
                (((1,), (1,)), ((), ())), preferred_element_type=F32,
            )
        terms.append(acc)
    r0[...] = jnp.concatenate(terms, axis=1).reshape(8, NZH, NY, 128)

    for o in range(1, 8):
        other, where = at_a(o)
        put(r0.at[other], ra.at[o - 1], ra_send.at[o - 1], ra_recv.at[o - 1], **where)
    part = r0[idx_a]
    for o in range(1, 8):
        arrived(ra.at[o - 1], ra_recv.at[o - 1])
    for o in range(1, 8):
        part += ra[o - 1]
    for q in range(16):
        rbs[q] = part[q // NY, q % NY : q % NY + 1, :]
    for o in (8, 12, 4, 7, 9, 11, 13, 5, 3, 6, 10, 14, 2, 15, 1):
        other = lax.rem(idx_b + o, 16)
        put(rbs.at[other], rb.at[o - 1], rb_send.at[o - 1], rb_recv.at[o - 1], zh=other // NY, y=lax.rem(other, NY))
    total = rbs[idx_b]
    for o in range(1, 16):
        arrived(rb.at[o - 1], rb_recv.at[o - 1])
    for o in range(1, 16):
        total += rb[o - 1]
    for n in range(BB):
        o_ref[n] = total[:, n * NA : (n + 1) * NA]

    @pl.when(zl == 0)
    def _():
        for s in range(8):
            left(piece, z_send.at[s])

    @pl.when(zl == 4)
    def _():
        for s in range(7):
            left(far_own, z_send.at[s])

    for o in range(NZL - 1):
        left(t_ref, t_send.at[o])
    for o in range(NX - 1):
        left(near_own, xn_send.at[o])
    for s in range(14):
        left(near_half(0, 0), yr_send.at[s])
    for o in range(NY - 1):
        left(far_own, yf_send.at[o])
    for s in range(6):
        left(far_half(0, 0), xf_send.at[s])
    for s in range(8):
        left(near_part(0), pn_send.at[s])
        left(far_half(0, 0), pf_send.at[s])
    for o in range(7):
        left(r0.at[0], ra_send.at[o])
    for o in range(15):
        left(rbs.at[0], rb_send.at[o])


def body(factors, amplitudes):
    dma = pltpu.SemaphoreType.DMA
    return pl.pallas_call(
        kernel,
        out_shape=jax.ShapeDtypeStruct((BB, 1, NA), F32),
        in_specs=[pl.BlockSpec(memory_space=pltpu.VMEM)] * 2,
        out_specs=pl.BlockSpec(memory_space=pltpu.VMEM),
        scratch_shapes=[
            pltpu.VMEM((8, AUX), BF),
            pltpu.VMEM((16, 4, NC, 8, AUX), BF),
            pltpu.VMEM((NZL, NY, NC, NCV, V), BF),
            pltpu.VMEM((NCV * NA, AUX), BF),
            pltpu.VMEM((NCV * PAIRS, V), BF),
            pltpu.VMEM((8, V, BB * 128), BF),
            pltpu.VMEM((BB, NCV * PAIRS, 1024), BF),
            pltpu.VMEM((NCV * NA, 1024), BF),
            pltpu.VMEM((8, NZH, NY, 128), F32),
            pltpu.VMEM((7, NZH, NY, 128), F32),
            pltpu.VMEM((16, 1, 128), F32),
            pltpu.VMEM((15, 1, 128), F32),
            dma((2,)), pltpu.SemaphoreType.REGULAR, dma((8,)), dma((2,)), dma((7,)), dma((7,)), dma((3,)), dma((3,)), dma((14,)), dma((14,)), dma((7,)),
            dma((7,)), dma((6,)), dma((6,)), dma((8,)), dma((8,)), dma((8,)), dma((8,)), dma((7,)), dma((7,)), dma((15,)), dma((15,)),
        ],
        compiler_params=pltpu.CompilerParams(collective_id=0, has_side_effects=True),
    )(factors, amplitudes.reshape(NY, NC, NCV, V))


def solution(mesh):
    torus = Mesh(mesh.devices.reshape(NZH, NX, NY, NC, NZL), (ZH, X, Y, CORE, ZL))
    in_specs = (P(ZL, VIR, None), P(ZL, VIR, None))
    return jax.shard_map(body, mesh=torus, in_specs=in_specs, out_specs=P(None, VIR, ZL), check_vma=False)
```

```python
import jax
import jax.numpy as jnp
from jax import lax
from jax.experimental import pallas as pl
from jax.experimental.pallas import tpu as pltpu
from jax.sharding import Mesh
from jax.sharding import PartitionSpec as P

ZH, X, Y, CORE, ZL = "vir_0", "vir_1", "vir_2", "vir_3", "out"
VIR = (ZH, X, Y, CORE)
NZH, NX, NY, NC, NZL = 2, 4, 8, 2, 8
BB, NCV, NA, AUX, V, PAIRS = 2, 4, 64, 1536, 512, 128
MESH = pl.DeviceIdType.MESH
BF, F32 = jnp.bfloat16, jnp.float32


def kernel(
    f_ref, t_ref, o_ref,
    piece, slab, traw, fm, tm, pick, te, integ, r0, ra, rbs, rb,
    local_sem, mid_sem, z_send, z_recv, t_send, t_recv, xn_send, xn_recv, yr_send, yr_recv,
    yf_send, yf_recv, xf_send, xf_recv, pn_send, pn_recv, pf_send, pf_recv,
    ra_send, ra_recv, rb_send, rb_recv,
):
    zh, x, y, h, zl = (lax.axis_index(n) for n in (ZH, X, Y, CORE, ZL))
    near = jnp.where(zl <= NZL // 2, zh, 1 - zh)
    names = {"zh": ZH, "x": X, "y": Y, "h": CORE, "zl": ZL}

    def to(where):
        return dict(device_id={names[k]: v for k, v in where.items()}, device_id_type=MESH)

    def put(src, dst, ssem, rsem, **where):
        pltpu.make_async_remote_copy(src_ref=src, dst_ref=dst, send_sem=ssem, recv_sem=rsem, **to(where)).start()

    def arrived(dst, rsem):
        pltpu.make_async_copy(dst, dst, rsem).wait()

    left = arrived

    barrier = pltpu.get_barrier_semaphore()
    idx_z = zh * NZL + zl
    idx_a = h * NX + x
    idx_b = zh * NY + y

    def at_z(o):
        other = lax.rem(idx_z + o + 16, 16)
        return dict(zh=other // NZL, zl=lax.rem(other, NZL))

    def at_a(o):
        other = lax.rem(idx_a + o, 8)
        return other, dict(h=other // NX, x=lax.rem(other, NX))

    for o in (-4, 4, -3, 3, -2, 2, -1, 1):
        pl.semaphore_signal(barrier, inc=1, **to(at_z(o)))
    for o in range(1, 8):
        pl.semaphore_signal(barrier, inc=1, **to(at_a(o)[1]))
    for o in range(1, NY):
        pl.semaphore_signal(barrier, inc=1, **to(dict(y=lax.rem(y + o, NY))))

    piece[0:4, :] = f_ref[0]
    piece[4:8, :] = f_ref[1]
    own_t = pltpu.make_async_copy(t_ref, traw.at[zl], local_sem.at[0])
    own_t.start()

    pl.semaphore_wait(barrier, 8 + 7 + 7)
    pl.semaphore_signal(mid_sem, inc=1, **to(at_z(-4)))

    near_own, far_own = slab.at[7, x, h], slab.at[8, 2, h]

    @pl.when(zl == 0)
    def _():
        own = pltpu.make_async_copy(piece, near_own, local_sem.at[1])
        own.start()
        put(piece, near_own, z_send.at[0], z_recv.at[0], **at_z(4))
        put(piece, far_own, z_send.at[1], z_recv.at[1], **at_z(-4))
        for s, o in enumerate((3, -3, 2, -2, 1, -1)):
            put(piece, near_own, z_send.at[2 + s], z_recv.at[0], **at_z(o))
        own.wait()

    for c in range(NCV):
        fm[c * NA : (c + 1) * NA, :] = f_ref[:, c, :]
    d = lax.broadcasted_iota(jnp.int32, (V, 128), 0)
    for g in range(8):
        j = lax.broadcasted_iota(jnp.int32, (1, 128), 1) + g * 128
        pos, xx, core, b, i = j // 64, (j // 16) % 4, (j // 8) % 2, (j // 4) % 2, j % 4
        if g < 4:
            step = jnp.where(pos % 2 == 0, NY - 1 - pos // 2, pos // 2 + 1)
            yy = lax.rem(jnp.where(pos == 7, 0, step) + y, NY)
            src = ((near * NX + xx) * NY + yy) * NC + core
        else:
            yy = lax.rem((pos % 2) * 4 + xx + y + NY - 2, NY)
            src = (((1 - near) * NX + lax.rem(x + g - 4, NX)) * NY + yy) * NC + core
        for n in range(BB):
            want = jnp.where(b == n, src * NCV + i, -1)
            pick[g, :, n * 128 : (n + 1) * 128] = jnp.where(d == want, 1.0, 0.0).astype(BF)

    @pl.when(zl != 0)
    def _():
        arrived(near_own, z_recv.at[0])

    @pl.when(zl == 4)
    def _():
        for s, o in enumerate((4, 3, 2, 1)):
            put(near_own, far_own, z_send.at[s], z_recv.at[1], **at_z(o))

    for o in range(1, NX):
        put(near_own, near_own, xn_send.at[o - 1], xn_recv.at[o - 1], x=lax.rem(x + o, NX))

    mate = lax.rem(zl + 4, NZL)
    quad = [(zl // 4) * 4 + lax.rem(zl + o, 4) for o in range(1, 4)]

    def amplitudes_out():
        put(t_ref, traw.at[zl], t_send.at[0], t_recv.at[0], zl=mate)
        for o in range(3):
            put(t_ref, traw.at[zl], t_send.at[1 + o], t_recv.at[1 + o], zl=quad[o])

    def amplitudes_on():
        arrived(t_ref, t_recv.at[0])
        for o in range(3):
            put(traw.at[mate], traw.at[mate], t_send.at[4 + o], t_recv.at[4 + o], zl=quad[o])

    up, down = lax.rem(y + 1, NY), lax.rem(y + NY - 1, NY)
    xup, xdown = lax.rem(x + 1, NX), lax.rem(x + NX - 1, NX)

    def near_part(pos):
        return slab.at[pos, :, h]

    def near_half(pos, f):
        return slab.at[pos, 2 * f : 2 * f + 2, h]

    def ring(src, dst, f, y_to):
        s = 2 * dst + f
        put(near_half(src, f), near_half(dst, f), yr_send.at[s], yr_recv.at[s], y=y_to)

    def ring_arrived(pos, f):
        arrived(near_half(pos, f), yr_recv.at[2 * pos + f])

    def share_near(pos):
        put(near_part(pos), near_part(pos), pn_send.at[pos], pn_recv.at[pos], h=1 - h)

    def near_shared(pos):
        arrived(near_part(pos), pn_recv.at[pos])

    def far_chunk(k, m):
        first = (2, 0, 0, 2)[m]
        return slab.at[8 + 2 * k + m // 2, first : first + 2, h]

    def far_on(src, dst, m, x_to):
        s = 4 * (dst - 1) + m
        put(far_chunk(src, m), far_chunk(dst, m), xf_send.at[s], xf_recv.at[s], x=x_to)

    def far_arrived(k, m):
        arrived(far_chunk(k, m), xf_recv.at[4 * (k - 1) + m])

    def share_far(k, m):
        s = 4 * k + m
        put(far_chunk(k, m), far_chunk(k, m), pf_send.at[s], pf_recv.at[s], h=1 - h)

    def far_shared(k):
        for m in range(4):
            arrived(far_chunk(k, m), pf_recv.at[4 * k + m])

    def multiply(g):
        rows = slab[2 * g : 2 * g + 2].reshape(128, AUX)
        tile = lax.dot_general(fm[...], rows, (((1,), (1,)), ((), ())), preferred_element_type=F32)
        integ[:, g * 128 : (g + 1) * 128] = tile.astype(BF)

    amplitudes_out()
    for o in range(1, NX):
        arrived(near_own, xn_recv.at[o - 1])
    for f in range(2):
        ring(7, 0, f, up)
        ring(7, 1, f, down)
    share_near(7)

    arrived(far_own, z_recv.at[1])

    @pl.when(zl == 4)
    def _():
        for s, o in enumerate((-3, -2, -1)):
            put(far_own, far_own, z_send.at[4 + s], z_recv.at[1], **at_z(o))

    pl.semaphore_wait(mid_sem, 1)

    def far_place(o):
        q = (2 - o) % NY
        return slab.at[8 + q // 4, q % 4, h]

    for o in (4, 7, 1, 3, 2, 6, 5):
        put(far_own, far_place(o), yf_send.at[o - 1], yf_recv.at[o - 1], y=lax.rem(y + o, NY))

    def ring_on(step):
        for f in range(2):
            ring_arrived(2 * step, f)
            ring(2 * step, 2 * step + 2, f, up)
            ring_arrived(2 * step + 1, f)
            ring(2 * step + 1, 2 * step + 3, f, down)
        share_near(2 * step)
        share_near(2 * step + 1)

    def column_on(m, *offsets):
        for o in offsets:
            arrived(far_own, yf_recv.at[o - 1])
        if m == 3:
            far_on(0, 2, m, lax.rem(x + 2, NX))
        far_on(0, 3, m, xup)
        far_on(0, 1, m, xdown)
        share_far(0, m)

    def rows_on(m):
        first, second, x_to = (3, 1, xup) if m % 2 == 0 else (1, 3, xdown)
        far_arrived(first, m)
        if m < 3:
            far_on(first, 2, m, x_to)
        share_far(first, m)
        far_arrived(second, m)
        share_far(second, m)

    def gather_pairs(half):
        for sx in range(NX):
            for core in range(NC):
                for c in range(NCV):
                    row = c * 64 + core * 32 + sx * 8
                    tm[row : row + 8, :] = traw[half * NX + sx, :, core, c, :]

    def expand(half, groups):
        for g in groups:
            spread = jnp.dot(tm[...], pick[g], preferred_element_type=F32).astype(BF)
            for c in range(NCV):
                for n in range(BB):
                    te[c, half, n, :, g * 128 : (g + 1) * 128] = spread[c * 64 : (c + 1) * 64, n * 128 : (n + 1) * 128]

    ring_on(0)
    column_on(0, 7)
    column_on(1, 1, 2)
    amplitudes_on()
    own_t.wait()
    for o in range(1, 4):
        arrived(t_ref, t_recv.at[o])
    gather_pairs(zl // 4)
    expand(zl // 4, range(4))
    ring_on(1)
    column_on(2, 6, 5)
    expand(zl // 4, range(4, 8))
    rows_on(0)
    column_on(3, 3, 4)
    near_shared(0)
    near_shared(1)
    multiply(0)
    rows_on(1)
    ring_arrived(4, 0)
    ring(4, 6, 0, up)
    ring_arrived(5, 1)
    ring(5, 6, 1, down)
    far_shared(0)
    multiply(4)
    rows_on(2)
    ring_arrived(4, 1)
    ring_arrived(5, 0)
    share_near(4)
    share_near(5)
    near_shared(2)
    near_shared(3)
    multiply(1)
    rows_on(3)
    for o in range(4, NZL - 1):
        arrived(t_ref, t_recv.at[o])
    gather_pairs(1 - zl // 4)
    expand(1 - zl // 4, range(4))
    for m in range(2):
        far_arrived(2, m)
        share_far(2, m)
    ring_arrived(6, 0)
    ring_arrived(6, 1)
    share_near(6)
    expand(1 - zl // 4, range(4, 8))
    for m in range(2, 4):
        far_arrived(2, m)
        share_far(2, m)
    near_shared(4)
    near_shared(5)
    multiply(2)
    for k in (1, 3):
        far_shared(k)
        multiply(4 + k)

    def terms(lo, hi):
        return sum(
            lax.dot_general(
                te[c, :, :, :, lo:hi].reshape(BB * PAIRS, hi - lo), integ[c * NA : (c + 1) * NA, lo:hi],
                (((1,), (1,)), ((), ())), preferred_element_type=F32,
            )
            for c in range(NCV)
        )

    acc = terms(0, 384) + terms(512, 768) + terms(896, 1024)
    near_shared(6)
    near_shared(7)
    multiply(3)
    far_shared(2)
    multiply(6)
    acc = (acc + terms(384, 512) + terms(768, 896)).reshape(NZH, BB, 8, NY, NA)
    for z in range(NZH):
        r0[:, z] = jnp.concatenate([acc[z, n] for n in range(BB)], axis=-1)

    for o in range(1, 8):
        other, where = at_a(o)
        put(r0.at[other], ra.at[o - 1], ra_send.at[o - 1], ra_recv.at[o - 1], **where)
    part = r0[idx_a]
    for o in range(1, 8):
        arrived(ra.at[o - 1], ra_recv.at[o - 1])
    for o in range(1, 8):
        part += ra[o - 1]
    for q in range(16):
        rbs[q] = part[q // NY, q % NY : q % NY + 1, :]
    for o in (8, 12, 4, 7, 9, 11, 13, 5, 3, 6, 10, 14, 2, 15, 1):
        other = lax.rem(idx_b + o, 16)
        put(rbs.at[other], rb.at[o - 1], rb_send.at[o - 1], rb_recv.at[o - 1], zh=other // NY, y=lax.rem(other, NY))
    total = rbs[idx_b]
    for o in range(1, 16):
        arrived(rb.at[o - 1], rb_recv.at[o - 1])
    for o in range(1, 16):
        total += rb[o - 1]
    for n in range(BB):
        o_ref[n] = total[:, n * NA : (n + 1) * NA]

    @pl.when(zl == 0)
    def _():
        for s in range(8):
            left(piece, z_send.at[s])

    @pl.when(zl == 4)
    def _():
        for s in range(7):
            left(far_own, z_send.at[s])

    for o in range(NZL - 1):
        left(t_ref, t_send.at[o])
    for o in range(NX - 1):
        left(near_own, xn_send.at[o])
    for s in range(14):
        left(near_half(0, 0), yr_send.at[s])
    for o in range(NY - 1):
        left(far_own, yf_send.at[o])
    for s in range(12):
        left(far_chunk(0, 0), xf_send.at[s])
    for s in range(8):
        left(near_part(0), pn_send.at[s])
    for s in range(16):
        left(far_chunk(0, 0), pf_send.at[s])
    for o in range(7):
        left(r0.at[0], ra_send.at[o])
    for o in range(15):
        left(rbs.at[0], rb_send.at[o])


def body(factors, amplitudes):
    dma = pltpu.SemaphoreType.DMA
    return pl.pallas_call(
        kernel,
        out_shape=jax.ShapeDtypeStruct((BB, 1, NA), F32),
        in_specs=[pl.BlockSpec(memory_space=pltpu.VMEM)] * 2,
        out_specs=pl.BlockSpec(memory_space=pltpu.VMEM),
        scratch_shapes=[
            pltpu.VMEM((8, AUX), BF),
            pltpu.VMEM((16, 4, NC, 8, AUX), BF),
            pltpu.VMEM((NZL, NY, NC, NCV, V), BF),
            pltpu.VMEM((NCV * NA, AUX), BF),
            pltpu.VMEM((NCV * 64, V), BF),
            pltpu.VMEM((8, V, BB * 128), BF),
            pltpu.VMEM((NCV, NZH, BB, 64, 1024), BF),
            pltpu.VMEM((NCV * NA, 1024), BF),
            pltpu.VMEM((8, NZH, NY, 128), F32),
            pltpu.VMEM((7, NZH, NY, 128), F32),
            pltpu.VMEM((16, 1, 128), F32),
            pltpu.VMEM((15, 1, 128), F32),
            dma((2,)), pltpu.SemaphoreType.REGULAR, dma((8,)), dma((2,)), dma((7,)), dma((7,)), dma((3,)), dma((3,)), dma((14,)), dma((14,)), dma((7,)),
            dma((7,)), dma((12,)), dma((12,)), dma((8,)), dma((8,)), dma((16,)), dma((16,)), dma((7,)), dma((7,)), dma((15,)), dma((15,)),
        ],
        compiler_params=pltpu.CompilerParams(collective_id=0, has_side_effects=True),
    )(factors, amplitudes.reshape(NY, NC, NCV, V))


def solution(mesh):
    torus = Mesh(mesh.devices.reshape(NZH, NX, NY, NC, NZL), (ZH, X, Y, CORE, ZL))
    in_specs = (P(ZL, VIR, None), P(ZL, VIR, None))
    return jax.shard_map(body, mesh=torus, in_specs=in_specs, out_specs=P(None, VIR, ZL), check_vma=False)
```

```python
import jax
import jax.numpy as jnp
from jax import lax
from jax.experimental import pallas as pl
from jax.experimental.pallas import tpu as pltpu
from jax.sharding import Mesh
from jax.sharding import PartitionSpec as P

ZH, X, Y, CORE, ZL = "vir_0", "vir_1", "vir_2", "vir_3", "out"
VIR = (ZH, X, Y, CORE)
NZH, NX, NY, NC, NZL = 2, 4, 8, 2, 8
BB, NCV, NA, AUX, V, PAIRS = 2, 4, 64, 1536, 512, 128
MESH = pl.DeviceIdType.MESH
BF, F32 = jnp.bfloat16, jnp.float32


def kernel(
    f_hbm, t_hbm, o_ref,
    f_ref, piece, slab, traw, fm, tm, pick, te, integ, r0, ra, rbs, rb,
    local_sem, mid_sem, z_send, z_recv, t_send, t_recv, xn_send, xn_recv, yr_send, yr_recv,
    yf_send, yf_recv, xf_send, xf_recv, pn_send, pn_recv, pf_send, pf_recv,
    ra_send, ra_recv, rb_send, rb_recv,
):
    zh, x, y, h, zl = (lax.axis_index(n) for n in (ZH, X, Y, CORE, ZL))
    near = jnp.where(zl <= NZL // 2, zh, 1 - zh)
    names = {"zh": ZH, "x": X, "y": Y, "h": CORE, "zl": ZL}

    def to(where):
        return dict(device_id={names[k]: v for k, v in where.items()}, device_id_type=MESH)

    def put(src, dst, ssem, rsem, **where):
        pltpu.make_async_remote_copy(src_ref=src, dst_ref=dst, send_sem=ssem, recv_sem=rsem, **to(where)).start()

    def arrived(dst, rsem):
        pltpu.make_async_copy(dst, dst, rsem).wait()

    left = arrived

    barrier = pltpu.get_barrier_semaphore()
    idx_z = zh * NZL + zl
    idx_a = h * NX + x
    idx_b = zh * NY + y

    def at_z(o):
        other = lax.rem(idx_z + o + 16, 16)
        return dict(zh=other // NZL, zl=lax.rem(other, NZL))

    def at_a(o):
        other = lax.rem(idx_a + o, 8)
        return other, dict(h=other // NX, x=lax.rem(other, NX))

    for o in (-4, 4, -3, 3, -2, 2, -1, 1):
        pl.semaphore_signal(barrier, inc=1, **to(at_z(o)))
    for o in range(1, 8):
        pl.semaphore_signal(barrier, inc=1, **to(at_a(o)[1]))
    for o in range(1, NY):
        pl.semaphore_signal(barrier, inc=1, **to(dict(y=lax.rem(y + o, NY))))

    own_f = pltpu.make_async_copy(f_hbm, f_ref, local_sem.at[2])
    own_f.start()
    t_ref = traw.at[zl]
    own_t = pltpu.make_async_copy(t_hbm, t_ref, local_sem.at[0])
    own_t.start()
    own_f.wait()
    piece[0:4, :] = f_ref[0]
    piece[4:8, :] = f_ref[1]
    own_t.wait()

    pl.semaphore_wait(barrier, 8 + 7 + 7)
    pl.semaphore_signal(mid_sem, inc=1, **to(at_z(-4)))

    near_own, far_own = slab.at[7, x, h], slab.at[8, 2, h]

    @pl.when(zl == 0)
    def _():
        own = pltpu.make_async_copy(piece, near_own, local_sem.at[1])
        own.start()
        put(piece, near_own, z_send.at[0], z_recv.at[0], **at_z(4))
        put(piece, far_own, z_send.at[1], z_recv.at[1], **at_z(-4))
        for s, o in enumerate((3, -3, 2, -2, 1, -1)):
            put(piece, near_own, z_send.at[2 + s], z_recv.at[0], **at_z(o))
        own.wait()

    for c in range(NCV):
        fm[c * NA : (c + 1) * NA, :] = f_ref[:, c, :]
    d = lax.broadcasted_iota(jnp.int32, (V, 128), 0)
    for g in range(8):
        j = lax.broadcasted_iota(jnp.int32, (1, 128), 1) + g * 128
        pos, xx, core, b, i = j // 64, (j // 16) % 4, (j // 8) % 2, (j // 4) % 2, j % 4
        if g < 4:
            step = jnp.where(pos % 2 == 0, NY - 1 - pos // 2, pos // 2 + 1)
            yy = lax.rem(jnp.where(pos == 7, 0, step) + y, NY)
            src = ((near * NX + xx) * NY + yy) * NC + core
        else:
            yy = lax.rem((pos % 2) * 4 + xx + y + NY - 2, NY)
            src = (((1 - near) * NX + lax.rem(x + g - 4, NX)) * NY + yy) * NC + core
        for n in range(BB):
            want = jnp.where(b == n, src * NCV + i, -1)
            pick[g, :, n * 128 : (n + 1) * 128] = jnp.where(d == want, 1.0, 0.0).astype(BF)

    @pl.when(zl != 0)
    def _():
        arrived(near_own, z_recv.at[0])

    @pl.when(zl == 4)
    def _():
        for s, o in enumerate((4, 3, 2, 1)):
            put(near_own, far_own, z_send.at[s], z_recv.at[1], **at_z(o))

    for o in range(1, NX):
        put(near_own, near_own, xn_send.at[o - 1], xn_recv.at[o - 1], x=lax.rem(x + o, NX))

    mate = lax.rem(zl + 4, NZL)
    quad = [(zl // 4) * 4 + lax.rem(zl + o, 4) for o in range(1, 4)]

    def amplitudes_out():
        put(t_ref, traw.at[zl], t_send.at[0], t_recv.at[0], zl=mate)
        for o in range(3):
            put(t_ref, traw.at[zl], t_send.at[1 + o], t_recv.at[1 + o], zl=quad[o])

    def amplitudes_on():
        arrived(t_ref, t_recv.at[0])
        for o in range(3):
            put(traw.at[mate], traw.at[mate], t_send.at[4 + o], t_recv.at[4 + o], zl=quad[o])

    up, down = lax.rem(y + 1, NY), lax.rem(y + NY - 1, NY)
    xup, xdown = lax.rem(x + 1, NX), lax.rem(x + NX - 1, NX)

    def near_part(pos):
        return slab.at[pos, :, h]

    def near_half(pos, f):
        return slab.at[pos, 2 * f : 2 * f + 2, h]

    def ring(src, dst, f, y_to):
        s = 2 * dst + f
        put(near_half(src, f), near_half(dst, f), yr_send.at[s], yr_recv.at[s], y=y_to)

    def ring_arrived(pos, f):
        arrived(near_half(pos, f), yr_recv.at[2 * pos + f])

    def share_near(pos):
        put(near_part(pos), near_part(pos), pn_send.at[pos], pn_recv.at[pos], h=1 - h)

    def near_shared(pos):
        arrived(near_part(pos), pn_recv.at[pos])

    def far_chunk(k, m):
        first = (2, 0, 0, 2)[m]
        return slab.at[8 + 2 * k + m // 2, first : first + 2, h]

    def far_on(src, dst, m, x_to):
        s = 4 * (dst - 1) + m
        put(far_chunk(src, m), far_chunk(dst, m), xf_send.at[s], xf_recv.at[s], x=x_to)

    def far_arrived(k, m):
        arrived(far_chunk(k, m), xf_recv.at[4 * (k - 1) + m])

    def share_far(k, m):
        s = 4 * k + m
        put(far_chunk(k, m), far_chunk(k, m), pf_send.at[s], pf_recv.at[s], h=1 - h)

    def far_shared(k):
        for m in range(4):
            arrived(far_chunk(k, m), pf_recv.at[4 * k + m])

    def multiply(g):
        rows = slab[2 * g : 2 * g + 2].reshape(128, AUX)
        tile = lax.dot_general(fm[...], rows, (((1,), (1,)), ((), ())), preferred_element_type=F32)
        integ[:, g * 128 : (g + 1) * 128] = tile.astype(BF)

    amplitudes_out()
    for o in range(1, NX):
        arrived(near_own, xn_recv.at[o - 1])
    for f in range(2):
        ring(7, 0, f, up)
        ring(7, 1, f, down)
    share_near(7)

    arrived(far_own, z_recv.at[1])

    @pl.when(zl == 4)
    def _():
        for s, o in enumerate((-3, -2, -1)):
            put(far_own, far_own, z_send.at[4 + s], z_recv.at[1], **at_z(o))

    pl.semaphore_wait(mid_sem, 1)

    def far_place(o):
        q = (2 - o) % NY
        return slab.at[8 + q // 4, q % 4, h]

    for o in (4, 7, 1, 3, 2, 6, 5):
        put(far_own, far_place(o), yf_send.at[o - 1], yf_recv.at[o - 1], y=lax.rem(y + o, NY))

    def ring_on(step):
        for f in range(2):
            ring_arrived(2 * step, f)
            ring(2 * step, 2 * step + 2, f, up)
            ring_arrived(2 * step + 1, f)
            ring(2 * step + 1, 2 * step + 3, f, down)
        share_near(2 * step)
        share_near(2 * step + 1)

    def column_on(m, *offsets):
        for o in offsets:
            arrived(far_own, yf_recv.at[o - 1])
        if m >= 2:
            far_on(0, 2, m, lax.rem(x + 2, NX))
        far_on(0, 3, m, xup)
        far_on(0, 1, m, xdown)
        share_far(0, m)

    def rows_on(m):
        first, second, x_to = (3, 1, xup) if m % 2 == 0 else (1, 3, xdown)
        far_arrived(first, m)
        if m < 2:
            far_on(first, 2, m, x_to)
        share_far(first, m)
        far_arrived(second, m)
        share_far(second, m)

    def gather_pairs(half):
        for sx in range(NX):
            for core in range(NC):
                for c in range(NCV):
                    row = c * 64 + core * 32 + sx * 8
                    tm[row : row + 8, :] = traw[half * NX + sx, :, core, c, :]

    def expand(half, groups):
        for g in groups:
            spread = jnp.dot(tm[...], pick[g], preferred_element_type=F32).astype(BF)
            for c in range(NCV):
                for n in range(BB):
                    te[c, half, n, :, g * 128 : (g + 1) * 128] = spread[c * 64 : (c + 1) * 64, n * 128 : (n + 1) * 128]

    ring_on(0)
    column_on(0, 7)
    column_on(1, 1, 2)
    amplitudes_on()
    for o in range(1, 4):
        arrived(t_ref, t_recv.at[o])
    gather_pairs(zl // 4)
    expand(zl // 4, range(4))
    ring_on(1)
    column_on(2, 6, 5)
    expand(zl // 4, range(4, 8))
    rows_on(0)
    column_on(3, 3, 4)
    near_shared(0)
    near_shared(1)
    multiply(0)
    rows_on(1)
    ring_arrived(4, 0)
    ring(4, 6, 0, up)
    ring_arrived(5, 1)
    ring(5, 6, 1, down)
    far_shared(0)
    multiply(4)
    rows_on(2)
    ring_arrived(4, 1)
    ring_arrived(5, 0)
    share_near(4)
    share_near(5)
    near_shared(2)
    near_shared(3)
    multiply(1)
    rows_on(3)
    for o in range(4, NZL - 1):
        arrived(t_ref, t_recv.at[o])
    gather_pairs(1 - zl // 4)
    expand(1 - zl // 4, range(4))
    for m in range(2):
        far_arrived(2, m)
        share_far(2, m)
    ring_arrived(6, 0)
    ring_arrived(6, 1)
    share_near(6)
    expand(1 - zl // 4, range(4, 8))
    for m in range(2, 4):
        far_arrived(2, m)
        share_far(2, m)
    near_shared(4)
    near_shared(5)
    multiply(2)
    for k in (1, 3):
        far_shared(k)
        multiply(4 + k)

    def terms(lo, hi):
        return sum(
            lax.dot_general(
                te[c, :, :, :, lo:hi].reshape(BB * PAIRS, hi - lo), integ[c * NA : (c + 1) * NA, lo:hi],
                (((1,), (1,)), ((), ())), preferred_element_type=F32,
            )
            for c in range(NCV)
        )

    acc = terms(0, 384) + terms(512, 768) + terms(896, 1024)
    near_shared(6)
    near_shared(7)
    multiply(3)
    far_shared(2)
    multiply(6)
    acc = (acc + terms(384, 512) + terms(768, 896)).reshape(NZH, BB, 8, NY, NA)
    for z in range(NZH):
        r0[:, z] = jnp.concatenate([acc[z, n] for n in range(BB)], axis=-1)

    for o in range(1, 8):
        other, where = at_a(o)
        put(r0.at[other], ra.at[o - 1], ra_send.at[o - 1], ra_recv.at[o - 1], **where)
    part = r0[idx_a]
    for o in range(1, 8):
        arrived(ra.at[o - 1], ra_recv.at[o - 1])
    for o in range(1, 8):
        part += ra[o - 1]
    for q in range(16):
        rbs[q] = part[q // NY, q % NY : q % NY + 1, :]
    for o in (12, 11, 13, 10, 14, 9, 15, 8, 4, 5, 3, 6, 2, 7, 1):
        other = lax.rem(idx_b + o, 16)
        put(rbs.at[other], rb.at[o - 1], rb_send.at[o - 1], rb_recv.at[o - 1], zh=other // NY, y=lax.rem(other, NY))
    @pl.when(zl == 0)
    def _():
        for s in range(8):
            left(piece, z_send.at[s])

    @pl.when(zl == 4)
    def _():
        for s in range(7):
            left(far_own, z_send.at[s])

    for o in range(NZL - 1):
        left(t_ref, t_send.at[o])
    for o in range(NX - 1):
        left(near_own, xn_send.at[o])
    for s in range(14):
        left(near_half(0, 0), yr_send.at[s])
    for o in range(NY - 1):
        left(far_own, yf_send.at[o])
    for s in range(12):
        left(far_chunk(0, 0), xf_send.at[s])
    for s in range(8):
        left(near_part(0), pn_send.at[s])
    for s in range(16):
        left(far_chunk(0, 0), pf_send.at[s])
    for o in range(7):
        left(r0.at[0], ra_send.at[o])

    for o in range(15):
        left(rbs.at[0], rb_send.at[o])
    total = rbs[idx_b]
    for o in range(1, 16):
        arrived(rb.at[o - 1], rb_recv.at[o - 1])
    for o in range(1, 16):
        total += rb[o - 1]
    for n in range(BB):
        o_ref[n] = total[:, n * NA : (n + 1) * NA]


def body(factors, amplitudes):
    dma = pltpu.SemaphoreType.DMA
    return pl.pallas_call(
        kernel,
        out_shape=jax.ShapeDtypeStruct((BB, 1, NA), F32),
        in_specs=[pl.BlockSpec(memory_space=pl.ANY)] * 2,
        out_specs=pl.BlockSpec(memory_space=pltpu.VMEM),
        scratch_shapes=[
            pltpu.VMEM((NA, NCV, AUX), BF),
            pltpu.VMEM((8, AUX), BF),
            pltpu.VMEM((16, 4, NC, 8, AUX), BF),
            pltpu.VMEM((NZL, NY, NC, NCV, V), BF),
            pltpu.VMEM((NCV * NA, AUX), BF),
            pltpu.VMEM((NCV * 64, V), BF),
            pltpu.VMEM((8, V, BB * 128), BF),
            pltpu.VMEM((NCV, NZH, BB, 64, 1024), BF),
            pltpu.VMEM((NCV * NA, 1024), BF),
            pltpu.VMEM((8, NZH, NY, 128), F32),
            pltpu.VMEM((7, NZH, NY, 128), F32),
            pltpu.VMEM((16, 1, 128), F32),
            pltpu.VMEM((15, 1, 128), F32),
            dma((3,)), pltpu.SemaphoreType.REGULAR, dma((8,)), dma((2,)), dma((7,)), dma((7,)), dma((3,)), dma((3,)), dma((14,)), dma((14,)), dma((7,)),
            dma((7,)), dma((12,)), dma((12,)), dma((8,)), dma((8,)), dma((16,)), dma((16,)), dma((7,)), dma((7,)), dma((15,)), dma((15,)),
        ],
        compiler_params=pltpu.CompilerParams(collective_id=0, has_side_effects=True),
    )(factors, amplitudes.reshape(NY, NC, NCV, V))


def solution(mesh):
    torus = Mesh(mesh.devices.reshape(NZH, NX, NY, NC, NZL), (ZH, X, Y, CORE, ZL))
    in_specs = (P(ZL, VIR, None), P(ZL, VIR, None))
    return jax.shard_map(body, mesh=torus, in_specs=in_specs, out_specs=P(None, VIR, ZL), check_vma=False)
```

```python
import jax
import jax.numpy as jnp
from jax import lax
from jax.experimental import pallas as pl
from jax.experimental.pallas import tpu as pltpu
from jax.sharding import Mesh
from jax.sharding import PartitionSpec as P

ZH, X, Y, CORE, ZL = "vir_0", "vir_1", "vir_2", "vir_3", "out"
VIR = (ZH, X, Y, CORE)
NZH, NX, NY, NC, NZL = 2, 4, 8, 2, 8
BB, NCV, NA, AUX, V, PAIRS = 2, 4, 64, 1536, 512, 128
MESH = pl.DeviceIdType.MESH
BF, F32 = jnp.bfloat16, jnp.float32


def kernel(
    f_hbm, t_hbm, o_ref,
    f_ref, piece, slab, traw, fm, tm, pick, te, integ, r0, ra, rbs, rb,
    local_sem, mid_sem, z_send, z_recv, t_send, t_recv, xn_send, xn_recv, yr_send, yr_recv,
    yf_send, yf_recv, xf_send, xf_recv, pn_send, pn_recv, pf_send, pf_recv,
    ra_send, ra_recv, rb_send, rb_recv,
):
    zh, x, y, h, zl = (lax.axis_index(n) for n in (ZH, X, Y, CORE, ZL))
    near = jnp.where(zl <= NZL // 2, zh, 1 - zh)
    names = {"zh": ZH, "x": X, "y": Y, "h": CORE, "zl": ZL}

    def to(where):
        return dict(device_id={names[k]: v for k, v in where.items()}, device_id_type=MESH)

    def put(src, dst, ssem, rsem, **where):
        pltpu.make_async_remote_copy(src_ref=src, dst_ref=dst, send_sem=ssem, recv_sem=rsem, **to(where)).start()

    def arrived(dst, rsem):
        pltpu.make_async_copy(dst, dst, rsem).wait()

    left = arrived

    barrier = pltpu.get_barrier_semaphore()
    idx_z = zh * NZL + zl
    idx_a = h * NX + x
    idx_b = zh * NY + y

    def at_z(o):
        other = lax.rem(idx_z + o + 16, 16)
        return dict(zh=other // NZL, zl=lax.rem(other, NZL))

    def at_a(o):
        other = lax.rem(idx_a + o, 8)
        return other, dict(h=other // NX, x=lax.rem(other, NX))

    for o in (-4, 4, -3, 3, -2, 2, -1, 1):
        pl.semaphore_signal(barrier, inc=1, **to(at_z(o)))
    for o in range(1, 8):
        pl.semaphore_signal(barrier, inc=1, **to(at_a(o)[1]))
    for o in range(1, NY):
        pl.semaphore_signal(barrier, inc=1, **to(dict(y=lax.rem(y + o, NY))))

    own_f = pltpu.make_async_copy(f_hbm, f_ref, local_sem.at[2])
    own_f.start()
    t_ref = traw.at[zl]
    own_t = pltpu.make_async_copy(t_hbm, t_ref, local_sem.at[0])
    own_t.start()
    own_f.wait()
    piece[0:4, :] = f_ref[0]
    piece[4:8, :] = f_ref[1]
    own_t.wait()

    pl.semaphore_wait(barrier, 8 + 7 + 7)
    pl.semaphore_signal(mid_sem, inc=1, **to(at_z(-4)))

    near_own, far_own = slab.at[7, x, h], slab.at[8, 2, h]

    @pl.when(zl == 0)
    def _():
        own = pltpu.make_async_copy(piece, near_own, local_sem.at[1])
        own.start()
        put(piece, near_own, z_send.at[0], z_recv.at[0], **at_z(4))
        put(piece, far_own, z_send.at[1], z_recv.at[1], **at_z(-4))
        for s, o in enumerate((3, -3, 2, -2, 1, -1)):
            put(piece, near_own, z_send.at[2 + s], z_recv.at[0], **at_z(o))
        own.wait()

    for c in range(NCV):
        fm[c * NA : (c + 1) * NA, :] = f_ref[:, c, :]
    d = lax.broadcasted_iota(jnp.int32, (V, 128), 0)
    for g in range(8):
        j = lax.broadcasted_iota(jnp.int32, (1, 128), 1) + g * 128
        pos, xx, core, b, i = j // 64, (j // 16) % 4, (j // 8) % 2, (j // 4) % 2, j % 4
        if g < 4:
            step = jnp.where(pos % 2 == 0, NY - 1 - pos // 2, pos // 2 + 1)
            yy = lax.rem(jnp.where(pos == 7, 0, step) + y, NY)
            src = ((near * NX + xx) * NY + yy) * NC + core
        else:
            yy = lax.rem((pos % 2) * 4 + xx + y + NY - 2, NY)
            src = (((1 - near) * NX + lax.rem(x + g - 4, NX)) * NY + yy) * NC + core
        for n in range(BB):
            want = jnp.where(b == n, src * NCV + i, -1)
            pick[g, :, n * 128 : (n + 1) * 128] = jnp.where(d == want, 1.0, 0.0).astype(BF)

    @pl.when(zl != 0)
    def _():
        arrived(near_own, z_recv.at[0])

    @pl.when(zl == 4)
    def _():
        for s, o in enumerate((4, 3, 2, 1)):
            put(near_own, far_own, z_send.at[s], z_recv.at[1], **at_z(o))
        arrived(far_own, z_recv.at[1])
        for s, o in enumerate((-3, -2, -1)):
            put(far_own, far_own, z_send.at[4 + s], z_recv.at[1], **at_z(o))

    for o in range(1, NX):
        put(near_own, near_own, xn_send.at[o - 1], xn_recv.at[o - 1], x=lax.rem(x + o, NX))

    mate = lax.rem(zl + 4, NZL)
    quad = [(zl // 4) * 4 + lax.rem(zl + o, 4) for o in range(1, 4)]

    def amplitudes_out():
        put(t_ref, traw.at[zl], t_send.at[0], t_recv.at[0], zl=mate)
        for o in range(3):
            put(t_ref, traw.at[zl], t_send.at[1 + o], t_recv.at[1 + o], zl=quad[o])

    def amplitudes_on():
        arrived(t_ref, t_recv.at[0])
        for o in range(3):
            put(traw.at[mate], traw.at[mate], t_send.at[4 + o], t_recv.at[4 + o], zl=quad[o])

    up, down = lax.rem(y + 1, NY), lax.rem(y + NY - 1, NY)
    xup, xdown = lax.rem(x + 1, NX), lax.rem(x + NX - 1, NX)

    def near_part(pos):
        return slab.at[pos, :, h]

    def near_half(pos, f):
        return slab.at[pos, 2 * f : 2 * f + 2, h]

    def ring(src, dst, f, y_to):
        s = 2 * dst + f
        put(near_half(src, f), near_half(dst, f), yr_send.at[s], yr_recv.at[s], y=y_to)

    def ring_arrived(pos, f):
        arrived(near_half(pos, f), yr_recv.at[2 * pos + f])

    def share_near(pos):
        put(near_part(pos), near_part(pos), pn_send.at[pos], pn_recv.at[pos], h=1 - h)

    def near_shared(pos):
        arrived(near_part(pos), pn_recv.at[pos])

    def far_chunk(k, m):
        first = (2, 0, 0, 2)[m]
        return slab.at[8 + 2 * k + m // 2, first : first + 2, h]

    def far_on(src, dst, m, x_to):
        s = 4 * (dst - 1) + m
        put(far_chunk(src, m), far_chunk(dst, m), xf_send.at[s], xf_recv.at[s], x=x_to)

    def far_arrived(k, m):
        arrived(far_chunk(k, m), xf_recv.at[4 * (k - 1) + m])

    def share_far(k, m):
        s = 4 * k + m
        put(far_chunk(k, m), far_chunk(k, m), pf_send.at[s], pf_recv.at[s], h=1 - h)

    def far_shared(k):
        for m in range(4):
            arrived(far_chunk(k, m), pf_recv.at[4 * k + m])

    def multiply(g):
        rows = slab[2 * g : 2 * g + 2].reshape(128, AUX)
        tile = lax.dot_general(fm[...], rows, (((1,), (1,)), ((), ())), preferred_element_type=F32)
        integ[:, g * 128 : (g + 1) * 128] = tile.astype(BF)

    amplitudes_out()
    for o in range(1, NX):
        arrived(near_own, xn_recv.at[o - 1])
    for f in range(2):
        ring(7, 0, f, up)
        ring(7, 1, f, down)
    share_near(7)

    @pl.when(zl != 4)
    def _():
        arrived(far_own, z_recv.at[1])

    pl.semaphore_wait(mid_sem, 1)

    def far_place(o):
        q = (2 - o) % NY
        return slab.at[8 + q // 4, q % 4, h]

    for o in (4, 7, 1, 3, 2, 6, 5):
        put(far_own, far_place(o), yf_send.at[o - 1], yf_recv.at[o - 1], y=lax.rem(y + o, NY))

    def ring_on(step):
        for f in range(2):
            ring_arrived(2 * step, f)
            ring(2 * step, 2 * step + 2, f, up)
            ring_arrived(2 * step + 1, f)
            ring(2 * step + 1, 2 * step + 3, f, down)
        share_near(2 * step)
        share_near(2 * step + 1)

    def column_on(m, *offsets):
        for o in offsets:
            arrived(far_own, yf_recv.at[o - 1])
        if m >= 2:
            far_on(0, 2, m, lax.rem(x + 2, NX))
        far_on(0, 3, m, xup)
        far_on(0, 1, m, xdown)
        share_far(0, m)

    def rows_on(m):
        first, second, x_to = (3, 1, xup) if m % 2 == 0 else (1, 3, xdown)
        far_arrived(first, m)
        if m < 2:
            far_on(first, 2, m, x_to)
        share_far(first, m)
        far_arrived(second, m)
        share_far(second, m)

    def gather_pairs(half):
        for sx in range(NX):
            for core in range(NC):
                for c in range(NCV):
                    row = c * 64 + core * 32 + sx * 8
                    tm[row : row + 8, :] = traw[half * NX + sx, :, core, c, :]

    def expand(half, groups):
        for g in groups:
            spread = jnp.dot(tm[...], pick[g], preferred_element_type=F32).astype(BF)
            for c in range(NCV):
                for n in range(BB):
                    te[c, half, n, :, g * 128 : (g + 1) * 128] = spread[c * 64 : (c + 1) * 64, n * 128 : (n + 1) * 128]

    ring_on(0)
    column_on(0, 7)
    column_on(1, 1, 2)
    amplitudes_on()
    for o in range(1, 4):
        arrived(t_ref, t_recv.at[o])
    gather_pairs(zl // 4)
    expand(zl // 4, range(4))
    ring_on(1)
    column_on(2, 6, 5)
    expand(zl // 4, range(4, 8))
    rows_on(0)
    column_on(3, 3, 4)
    near_shared(0)
    near_shared(1)
    multiply(0)
    rows_on(1)
    ring_arrived(4, 0)
    ring(4, 6, 0, up)
    ring_arrived(5, 1)
    ring(5, 6, 1, down)
    far_shared(0)
    multiply(4)
    rows_on(2)
    ring_arrived(4, 1)
    ring_arrived(5, 0)
    share_near(4)
    share_near(5)
    near_shared(2)
    near_shared(3)
    multiply(1)
    rows_on(3)
    for o in range(4, NZL - 1):
        arrived(t_ref, t_recv.at[o])
    gather_pairs(1 - zl // 4)
    expand(1 - zl // 4, range(4))
    for m in range(2):
        far_arrived(2, m)
        share_far(2, m)
    ring_arrived(6, 0)
    ring_arrived(6, 1)
    share_near(6)
    expand(1 - zl // 4, range(4, 8))
    for m in range(2, 4):
        far_arrived(2, m)
        share_far(2, m)
    near_shared(4)
    near_shared(5)
    multiply(2)
    for k in (1, 3):
        far_shared(k)
        multiply(4 + k)

    def terms(lo, hi):
        return sum(
            lax.dot_general(
                te[c, :, :, :, lo:hi].reshape(BB * PAIRS, hi - lo), integ[c * NA : (c + 1) * NA, lo:hi],
                (((1,), (1,)), ((), ())), preferred_element_type=F32,
            )
            for c in range(NCV)
        )

    acc = terms(0, 384) + terms(512, 768) + terms(896, 1024)
    near_shared(6)
    near_shared(7)
    multiply(3)
    far_shared(2)
    multiply(6)
    acc = (acc + terms(384, 512) + terms(768, 896)).reshape(NZH, BB, 8, NY, NA)
    for z in range(NZH):
        r0[:, z] = jnp.concatenate([acc[z, n] for n in range(BB)], axis=-1)

    for o in range(1, 8):
        other, where = at_a(o)
        put(r0.at[other], ra.at[o - 1], ra_send.at[o - 1], ra_recv.at[o - 1], **where)
    part = r0[idx_a]
    for o in range(1, 8):
        arrived(ra.at[o - 1], ra_recv.at[o - 1])
    for o in range(1, 8):
        part += ra[o - 1]
    for q in range(16):
        rbs[q] = part[q // NY, q % NY : q % NY + 1, :]
    for o in (12, 11, 13, 10, 14, 9, 15, 8, 4, 5, 3, 6, 2, 7, 1):
        other = lax.rem(idx_b + o, 16)
        put(rbs.at[other], rb.at[o - 1], rb_send.at[o - 1], rb_recv.at[o - 1], zh=other // NY, y=lax.rem(other, NY))
    @pl.when(zl == 0)
    def _():
        for s in range(8):
            left(piece, z_send.at[s])

    @pl.when(zl == 4)
    def _():
        for s in range(7):
            left(far_own, z_send.at[s])

    for o in range(NZL - 1):
        left(t_ref, t_send.at[o])
    for o in range(NX - 1):
        left(near_own, xn_send.at[o])
    for s in range(14):
        left(near_half(0, 0), yr_send.at[s])
    for o in range(NY - 1):
        left(far_own, yf_send.at[o])
    for s in range(12):
        left(far_chunk(0, 0), xf_send.at[s])
    for s in range(8):
        left(near_part(0), pn_send.at[s])
    for s in range(16):
        left(far_chunk(0, 0), pf_send.at[s])
    for o in range(7):
        left(r0.at[0], ra_send.at[o])

    for o in range(15):
        left(rbs.at[0], rb_send.at[o])
    total = rbs[idx_b]
    for o in range(1, 16):
        arrived(rb.at[o - 1], rb_recv.at[o - 1])
    for o in range(1, 16):
        total += rb[o - 1]
    for n in range(BB):
        o_ref[n] = total[:, n * NA : (n + 1) * NA]


def body(factors, amplitudes):
    dma = pltpu.SemaphoreType.DMA
    return pl.pallas_call(
        kernel,
        out_shape=jax.ShapeDtypeStruct((BB, 1, NA), F32),
        in_specs=[pl.BlockSpec(memory_space=pl.ANY)] * 2,
        out_specs=pl.BlockSpec(memory_space=pltpu.VMEM),
        scratch_shapes=[
            pltpu.VMEM((NA, NCV, AUX), BF),
            pltpu.VMEM((8, AUX), BF),
            pltpu.VMEM((16, 4, NC, 8, AUX), BF),
            pltpu.VMEM((NZL, NY, NC, NCV, V), BF),
            pltpu.VMEM((NCV * NA, AUX), BF),
            pltpu.VMEM((NCV * 64, V), BF),
            pltpu.VMEM((8, V, BB * 128), BF),
            pltpu.VMEM((NCV, NZH, BB, 64, 1024), BF),
            pltpu.VMEM((NCV * NA, 1024), BF),
            pltpu.VMEM((8, NZH, NY, 128), F32),
            pltpu.VMEM((7, NZH, NY, 128), F32),
            pltpu.VMEM((16, 1, 128), F32),
            pltpu.VMEM((15, 1, 128), F32),
            dma((3,)), pltpu.SemaphoreType.REGULAR, dma((8,)), dma((2,)), dma((7,)), dma((7,)), dma((3,)), dma((3,)), dma((14,)), dma((14,)), dma((7,)),
            dma((7,)), dma((12,)), dma((12,)), dma((8,)), dma((8,)), dma((16,)), dma((16,)), dma((7,)), dma((7,)), dma((15,)), dma((15,)),
        ],
        compiler_params=pltpu.CompilerParams(collective_id=0, has_side_effects=True),
    )(factors, amplitudes.reshape(NY, NC, NCV, V))


def solution(mesh):
    torus = Mesh(mesh.devices.reshape(NZH, NX, NY, NC, NZL), (ZH, X, Y, CORE, ZL))
    in_specs = (P(ZL, VIR, None), P(ZL, VIR, None))
    return jax.shard_map(body, mesh=torus, in_specs=in_specs, out_specs=P(None, VIR, ZL), check_vma=False)
```

```python
import jax
import jax.numpy as jnp
from jax import lax
from jax.experimental import pallas as pl
from jax.experimental.pallas import tpu as pltpu
from jax.sharding import Mesh
from jax.sharding import PartitionSpec as P

ZH, X, Y, CORE, ZL = "vir_0", "vir_1", "vir_2", "vir_3", "out"
VIR = (ZH, X, Y, CORE)
NZH, NX, NY, NC, NZL = 2, 4, 8, 2, 8
BB, NCV, NA, AUX, V, PAIRS = 2, 4, 64, 1536, 512, 128
MESH = pl.DeviceIdType.MESH
BF, F32 = jnp.bfloat16, jnp.float32


def kernel(
    f_hbm, t_hbm, o_ref,
    f_ref, piece, slab, traw, fm, tm, pick, te, integ, r0, ra, rbs, rb,
    local_sem, mid_sem, z_send, z_recv, t_send, t_recv, xn_send, xn_recv, yr_send, yr_recv,
    yf_send, yf_recv, xf_send, xf_recv, pn_send, pn_recv, pf_send, pf_recv,
    ra_send, ra_recv, rb_send, rb_recv,
):
    zh, x, y, h, zl = (lax.axis_index(n) for n in (ZH, X, Y, CORE, ZL))
    near = jnp.where(zl <= NZL // 2, zh, 1 - zh)
    names = {"zh": ZH, "x": X, "y": Y, "h": CORE, "zl": ZL}

    def to(where):
        return dict(device_id={names[k]: v for k, v in where.items()}, device_id_type=MESH)

    def put(src, dst, ssem, rsem, **where):
        pltpu.make_async_remote_copy(src_ref=src, dst_ref=dst, send_sem=ssem, recv_sem=rsem, **to(where)).start()

    def arrived(dst, rsem):
        pltpu.make_async_copy(dst, dst, rsem).wait()

    left = arrived

    barrier = pltpu.get_barrier_semaphore()
    idx_z = zh * NZL + zl
    idx_a = h * NX + x
    idx_b = zh * NY + y

    def at_z(o):
        other = lax.rem(idx_z + o + 16, 16)
        return dict(zh=other // NZL, zl=lax.rem(other, NZL))

    def at_a(o):
        other = lax.rem(idx_a + o, 8)
        return other, dict(h=other // NX, x=lax.rem(other, NX))

    for o in (-4, 4, -3, 3, -2, 2, -1, 1):
        pl.semaphore_signal(barrier, inc=1, **to(at_z(o)))
    for o in range(1, 8):
        pl.semaphore_signal(barrier, inc=1, **to(at_a(o)[1]))
    for o in range(1, NY):
        pl.semaphore_signal(barrier, inc=1, **to(dict(y=lax.rem(y + o, NY))))

    own_f = pltpu.make_async_copy(f_hbm, f_ref, local_sem.at[2])
    own_f.start()
    t_ref = traw.at[zl]
    own_t = pltpu.make_async_copy(t_hbm, t_ref, local_sem.at[0])
    own_t.start()
    own_f.wait()
    piece[0:4, :] = f_ref[0]
    piece[4:8, :] = f_ref[1]
    own_t.wait()

    pl.semaphore_wait(barrier, 8 + 7 + 7)
    pl.semaphore_signal(mid_sem, inc=1, **to(at_z(-4)))

    near_own, far_own = slab.at[7, x, h], slab.at[8, 2, h]

    @pl.when(zl == 0)
    def _():
        own = pltpu.make_async_copy(piece, near_own, local_sem.at[1])
        own.start()
        put(piece, near_own, z_send.at[0], z_recv.at[0], **at_z(4))
        put(piece, far_own, z_send.at[1], z_recv.at[1], **at_z(-4))
        for s, o in enumerate((3, -3, 2, -2, 1, -1)):
            put(piece, near_own, z_send.at[2 + s], z_recv.at[0], **at_z(o))
        own.wait()

    for c in range(NCV):
        fm[c * NA : (c + 1) * NA, :] = f_ref[:, c, :]
    d = lax.broadcasted_iota(jnp.int32, (V, 128), 0)
    for g in range(8):
        j = lax.broadcasted_iota(jnp.int32, (1, 128), 1) + g * 128
        pos, xx, core, b, i = j // 64, (j // 16) % 4, (j // 8) % 2, (j // 4) % 2, j % 4
        if g < 4:
            step = jnp.where(pos % 2 == 0, NY - 1 - pos // 2, pos // 2 + 1)
            yy = lax.rem(jnp.where(pos == 7, 0, step) + y, NY)
            src = ((near * NX + xx) * NY + yy) * NC + core
        else:
            yy = lax.rem((pos % 2) * 4 + xx + y + NY - 2, NY)
            src = (((1 - near) * NX + lax.rem(x + g - 4, NX)) * NY + yy) * NC + core
        for n in range(BB):
            want = jnp.where(b == n, src * NCV + i, -1)
            pick[g, :, n * 128 : (n + 1) * 128] = jnp.where(d == want, 1.0, 0.0).astype(BF)

    @pl.when(zl != 0)
    def _():
        arrived(near_own, z_recv.at[0])

    @pl.when(zl == 4)
    def _():
        for s, o in enumerate((4, 3, 2, 1)):
            put(near_own, far_own, z_send.at[s], z_recv.at[1], **at_z(o))
        arrived(far_own, z_recv.at[1])
        for s, o in enumerate((-3, -2, -1)):
            put(far_own, far_own, z_send.at[4 + s], z_recv.at[1], **at_z(o))

    for o in range(1, NX):
        put(near_own, near_own, xn_send.at[o - 1], xn_recv.at[o - 1], x=lax.rem(x + o, NX))

    mate = lax.rem(zl + 4, NZL)
    quad = [(zl // 4) * 4 + lax.rem(zl + o, 4) for o in range(1, 4)]

    def amplitudes_out():
        put(t_ref, traw.at[zl], t_send.at[0], t_recv.at[0], zl=mate)
        for o in range(3):
            put(t_ref, traw.at[zl], t_send.at[1 + o], t_recv.at[1 + o], zl=quad[o])

    def amplitudes_on():
        arrived(t_ref, t_recv.at[0])
        for o in range(3):
            put(traw.at[mate], traw.at[mate], t_send.at[4 + o], t_recv.at[4 + o], zl=quad[o])

    up, down = lax.rem(y + 1, NY), lax.rem(y + NY - 1, NY)
    xup, xdown = lax.rem(x + 1, NX), lax.rem(x + NX - 1, NX)

    def near_part(pos):
        return slab.at[pos, :, h]

    def near_half(pos, f):
        return slab.at[pos, 2 * f : 2 * f + 2, h]

    def ring(src, dst, f, y_to):
        s = 2 * dst + f
        put(near_half(src, f), near_half(dst, f), yr_send.at[s], yr_recv.at[s], y=y_to)

    def ring_arrived(pos, f):
        arrived(near_half(pos, f), yr_recv.at[2 * pos + f])

    def share_near(pos):
        put(near_part(pos), near_part(pos), pn_send.at[pos], pn_recv.at[pos], h=1 - h)

    def near_shared(pos):
        arrived(near_part(pos), pn_recv.at[pos])

    def far_chunk(k, m):
        first = (2, 0, 0, 2)[m]
        return slab.at[8 + 2 * k + m // 2, first : first + 2, h]

    def far_on(src, dst, m, x_to):
        s = 4 * (dst - 1) + m
        put(far_chunk(src, m), far_chunk(dst, m), xf_send.at[s], xf_recv.at[s], x=x_to)

    def far_arrived(k, m):
        arrived(far_chunk(k, m), xf_recv.at[4 * (k - 1) + m])

    def share_far(k, m):
        s = 4 * k + m
        put(far_chunk(k, m), far_chunk(k, m), pf_send.at[s], pf_recv.at[s], h=1 - h)

    def far_shared(k):
        for m in range(4):
            arrived(far_chunk(k, m), pf_recv.at[4 * k + m])

    def multiply(g):
        rows = slab[2 * g : 2 * g + 2].reshape(128, AUX)
        tile = lax.dot_general(fm[...], rows, (((1,), (1,)), ((), ())), preferred_element_type=F32)
        integ[:, g * 128 : (g + 1) * 128] = tile.astype(BF)

    amplitudes_out()
    for o in range(1, NX):
        arrived(near_own, xn_recv.at[o - 1])
    for f in range(2):
        ring(7, 0, f, up)
        ring(7, 1, f, down)
    share_near(7)

    @pl.when(zl != 4)
    def _():
        arrived(far_own, z_recv.at[1])

    pl.semaphore_wait(mid_sem, 1)

    def far_place(o):
        q = (2 - o) % NY
        return slab.at[8 + q // 4, q % 4, h]

    for o in (4, 7, 1, 3, 2, 6, 5):
        put(far_own, far_place(o), yf_send.at[o - 1], yf_recv.at[o - 1], y=lax.rem(y + o, NY))

    def ring_on(step):
        for f in range(2):
            ring_arrived(2 * step, f)
            ring(2 * step, 2 * step + 2, f, up)
            ring_arrived(2 * step + 1, f)
            ring(2 * step + 1, 2 * step + 3, f, down)
        share_near(2 * step)
        share_near(2 * step + 1)

    def column_on(m, *offsets):
        for o in offsets:
            arrived(far_own, yf_recv.at[o - 1])
        if m >= 2:
            far_on(0, 2, m, lax.rem(x + 2, NX))
        far_on(0, 3, m, xup)
        far_on(0, 1, m, xdown)
        share_far(0, m)

    def rows_on(m):
        first, second, x_to = (3, 1, xup) if m % 2 == 0 else (1, 3, xdown)
        far_arrived(first, m)
        if m < 2:
            far_on(first, 2, m, x_to)
        share_far(first, m)
        far_arrived(second, m)
        share_far(second, m)

    def gather_pairs(half):
        for sx in range(NX):
            for core in range(NC):
                for c in range(NCV):
                    row = c * 64 + core * 32 + sx * 8
                    tm[row : row + 8, :] = traw[half * NX + sx, :, core, c, :]

    def expand(half, groups):
        for g in groups:
            spread = jnp.dot(tm[...], pick[g], preferred_element_type=F32).astype(BF)
            for c in range(NCV):
                for n in range(BB):
                    te[c, half, n, :, g * 128 : (g + 1) * 128] = spread[c * 64 : (c + 1) * 64, n * 128 : (n + 1) * 128]

    ring_on(0)
    column_on(0, 7)
    column_on(1, 1, 2)
    amplitudes_on()
    for o in range(1, 4):
        arrived(t_ref, t_recv.at[o])
    gather_pairs(zl // 4)
    expand(zl // 4, range(4))
    ring_on(1)
    column_on(2, 6, 5)
    expand(zl // 4, range(4, 8))
    rows_on(0)
    column_on(3, 3, 4)
    near_shared(0)
    near_shared(1)
    multiply(0)
    rows_on(1)
    ring_arrived(4, 0)
    ring(4, 6, 0, up)
    ring_arrived(5, 1)
    ring(5, 6, 1, down)
    far_shared(0)
    multiply(4)
    rows_on(2)
    ring_arrived(4, 1)
    ring_arrived(5, 0)
    share_near(4)
    share_near(5)
    near_shared(2)
    near_shared(3)
    multiply(1)
    rows_on(3)
    near_shared(4)
    near_shared(5)
    multiply(2)
    for o in range(4, NZL - 1):
        arrived(t_ref, t_recv.at[o])
    gather_pairs(1 - zl // 4)
    expand(1 - zl // 4, range(4))
    for m in range(2):
        far_arrived(2, m)
        share_far(2, m)
    ring_arrived(6, 0)
    ring_arrived(6, 1)
    share_near(6)
    expand(1 - zl // 4, range(4, 8))
    for m in range(2, 4):
        far_arrived(2, m)
        share_far(2, m)
    for k in (1, 3):
        far_shared(k)
        multiply(4 + k)

    def terms(lo, hi):
        return sum(
            lax.dot_general(
                te[c, :, :, :, lo:hi].reshape(BB * PAIRS, hi - lo), integ[c * NA : (c + 1) * NA, lo:hi],
                (((1,), (1,)), ((), ())), preferred_element_type=F32,
            )
            for c in range(NCV)
        )

    acc = terms(0, 384) + terms(512, 768) + terms(896, 1024)
    near_shared(6)
    near_shared(7)
    multiply(3)
    far_shared(2)
    multiply(6)
    acc = (acc + terms(384, 512) + terms(768, 896)).reshape(NZH, BB, 8, NY, NA)
    for z in range(NZH):
        r0[:, z] = jnp.concatenate([acc[z, n] for n in range(BB)], axis=-1)

    for o in range(1, 8):
        other, where = at_a(o)
        put(r0.at[other], ra.at[o - 1], ra_send.at[o - 1], ra_recv.at[o - 1], **where)
    part = r0[idx_a]
    for o in range(1, 8):
        arrived(ra.at[o - 1], ra_recv.at[o - 1])
    for o in range(1, 8):
        part += ra[o - 1]
    for q in range(16):
        rbs[q] = part[q // NY, q % NY : q % NY + 1, :]
    for o in (12, 11, 13, 10, 14, 9, 15, 8, 4, 5, 3, 6, 2, 7, 1):
        other = lax.rem(idx_b + o, 16)
        put(rbs.at[other], rb.at[o - 1], rb_send.at[o - 1], rb_recv.at[o - 1], zh=other // NY, y=lax.rem(other, NY))
    @pl.when(zl == 0)
    def _():
        for s in range(8):
            left(piece, z_send.at[s])

    @pl.when(zl == 4)
    def _():
        for s in range(7):
            left(far_own, z_send.at[s])

    for o in range(NZL - 1):
        left(t_ref, t_send.at[o])
    for o in range(NX - 1):
        left(near_own, xn_send.at[o])
    for s in range(14):
        left(near_half(0, 0), yr_send.at[s])
    for o in range(NY - 1):
        left(far_own, yf_send.at[o])
    for s in range(12):
        left(far_chunk(0, 0), xf_send.at[s])
    for s in range(8):
        left(near_part(0), pn_send.at[s])
    for s in range(16):
        left(far_chunk(0, 0), pf_send.at[s])
    for o in range(7):
        left(r0.at[0], ra_send.at[o])

    for o in range(15):
        left(rbs.at[0], rb_send.at[o])
    total = rbs[idx_b]
    for o in range(1, 16):
        arrived(rb.at[o - 1], rb_recv.at[o - 1])
    for o in range(1, 16):
        total += rb[o - 1]
    for n in range(BB):
        o_ref[n] = total[:, n * NA : (n + 1) * NA]


def body(factors, amplitudes):
    dma = pltpu.SemaphoreType.DMA
    return pl.pallas_call(
        kernel,
        out_shape=jax.ShapeDtypeStruct((BB, 1, NA), F32),
        in_specs=[pl.BlockSpec(memory_space=pl.ANY)] * 2,
        out_specs=pl.BlockSpec(memory_space=pltpu.VMEM),
        scratch_shapes=[
            pltpu.VMEM((NA, NCV, AUX), BF),
            pltpu.VMEM((8, AUX), BF),
            pltpu.VMEM((16, 4, NC, 8, AUX), BF),
            pltpu.VMEM((NZL, NY, NC, NCV, V), BF),
            pltpu.VMEM((NCV * NA, AUX), BF),
            pltpu.VMEM((NCV * 64, V), BF),
            pltpu.VMEM((8, V, BB * 128), BF),
            pltpu.VMEM((NCV, NZH, BB, 64, 1024), BF),
            pltpu.VMEM((NCV * NA, 1024), BF),
            pltpu.VMEM((8, NZH, NY, 128), F32),
            pltpu.VMEM((7, NZH, NY, 128), F32),
            pltpu.VMEM((16, 1, 128), F32),
            pltpu.VMEM((15, 1, 128), F32),
            dma((3,)), pltpu.SemaphoreType.REGULAR, dma((8,)), dma((2,)), dma((7,)), dma((7,)), dma((3,)), dma((3,)), dma((14,)), dma((14,)), dma((7,)),
            dma((7,)), dma((12,)), dma((12,)), dma((8,)), dma((8,)), dma((16,)), dma((16,)), dma((7,)), dma((7,)), dma((15,)), dma((15,)),
        ],
        compiler_params=pltpu.CompilerParams(collective_id=0, has_side_effects=True),
    )(factors, amplitudes.reshape(NY, NC, NCV, V))


def solution(mesh):
    torus = Mesh(mesh.devices.reshape(NZH, NX, NY, NC, NZL), (ZH, X, Y, CORE, ZL))
    in_specs = (P(ZL, VIR, None), P(ZL, VIR, None))
    return jax.shard_map(body, mesh=torus, in_specs=in_specs, out_specs=P(None, VIR, ZL), check_vma=False)
```
